256 devices in a mesh: out: 16 (over x, z_lo, core), in: 16 (over z_hi, y).
Axes of the slice: x: 4, y: 4, z: 8 (z_hi: 4, z_lo: 2; z = z_hi * 2 + z_lo), core: 2. Of those that a mesh axis runs over, the one named last changes fastest.
Arguments:
- cotangent: bfloat16 [2048, 16384], P('in', 'out'), may hold values from -25.588427 to 25.588427
- activations: bfloat16 [2048, 16384], P('out', 'in'), may hold values from -1158 to 1158
- basis_out: bfloat16 [16384, 1024], P('out'), may hold values from -1 to 1, as said below
- basis_in: bfloat16 [16384, 1024], P('in'), may hold values from -1 to 1, as said below
Outputs:
- projected: float32 [16384, 16384], P('out', 'in')
The draws below stay inside these ranges and needn't reach their ends.
Inputs may be any that keep to these rules, and one draw needn't show every extreme that they name: The columns of basis_out are orthonormal before rounding to bfloat16. The columns of basis_in are orthonormal before rounding to bfloat16.
All inputs are finite; a program needn't handle non-finite values.
Results may differ from the reference program's by a relative error of at most 0.018.
Values may be sent and summed in bfloat16 or wider, within the bound.
A program may use at most 64 MiB of HBM per device.

```python
import math
import jax
import jax.numpy as jnp
from jax import lax

OUT = 16384
IN = 16384
RANK = 1024
TOKENS = 2048


def basis_matrix(key, row_total, stream):
    sub_key = jax.random.fold_in(key, stream)
    sample = jax.random.normal(sub_key, (row_total, RANK), jnp.float32)
    orthonormal, triangle = jnp.linalg.qr(sample)
    return orthonormal


def noise_field(key, stream, extent):
    sub_key = jax.random.fold_in(key, stream)
    return jax.random.truncated_normal(sub_key, -6.0, 6.0, extent, jnp.float32)


def draw_cotangent(key, part):
    strength = 5.0
    basis_rows = basis_matrix(key, OUT, 11)
    inside = jnp.dot(noise_field(key, 22, (TOKENS, RANK)), basis_rows.T, precision=lax.Precision.HIGHEST)
    result = (noise_field(key, 21, (TOKENS, OUT)) + strength * inside) / math.sqrt(TOKENS)
    return result.astype(jnp.bfloat16)


def draw_activations(key, part):
    strength = 5.0
    basis_rows = basis_matrix(key, IN, 12)
    inside = jnp.dot(noise_field(key, 32, (TOKENS, RANK)), basis_rows.T, precision=lax.Precision.HIGHEST)
    result = noise_field(key, 31, (TOKENS, IN)) + strength * inside
    return result.astype(jnp.bfloat16)


def draw_basis_out(key, part):
    return basis_matrix(key, OUT, 11).astype(jnp.bfloat16)


def draw_basis_in(key, part):
    return basis_matrix(key, IN, 12).astype(jnp.bfloat16)


def setup_inputs(seed: int = 0) -> dict:
    splits = jax.random.split(jax.random.key(seed), 5)
    cotangent = draw_cotangent(jax.random.fold_in(splits[4], 71), 0)
    activations = draw_activations(jax.random.fold_in(splits[4], 71), 0)
    basis_out = draw_basis_out(jax.random.fold_in(splits[4], 71), 0)
    basis_in = draw_basis_in(jax.random.fold_in(splits[4], 71), 0)
    return dict(cotangent=cotangent, activations=activations, basis_out=basis_out, basis_in=basis_in)


def reference(cotangent, activations, basis_out, basis_in):
    gradient = lax.dot_general(cotangent.astype(jnp.float32), activations.astype(jnp.float32), (((0,), (0,)), ((), ())), preferred_element_type=jnp.float32)
    gradient_low = gradient.astype(jnp.bfloat16)
    compressed = jnp.dot(gradient_low.astype(jnp.float32), basis_in.astype(jnp.float32), preferred_element_type=jnp.float32)
    core_matrix = lax.dot_general(basis_out.astype(jnp.float32), compressed.astype(jnp.bfloat16).astype(jnp.float32), (((0,), (0,)), ((), ())), preferred_element_type=jnp.float32)
    expansion = jnp.dot(basis_out.astype(jnp.float32), core_matrix.astype(jnp.bfloat16).astype(jnp.float32), preferred_element_type=jnp.float32).astype(jnp.bfloat16)
    removal = lax.dot_general(expansion.astype(jnp.float32), basis_in.astype(jnp.float32), (((1,), (1,)), ((), ())), preferred_element_type=jnp.float32)
    return gradient - removal
```

```python
import jax
import jax.numpy as jnp
from jax import lax
from jax.sharding import PartitionSpec as P

F32 = jnp.float32
BF16 = jnp.bfloat16


def body(cotangent, activations, basis_out, basis_in):
    ut = lax.dot_general(basis_out, cotangent, (((0,), (1,)), ((), ())), preferred_element_type=F32)
    vt = lax.dot_general(basis_in, activations, (((0,), (1,)), ((), ())), preferred_element_type=F32)
    ut = lax.psum_scatter(ut.astype(BF16), "out", scatter_dimension=0, tiled=True)
    vt = lax.psum_scatter(vt.astype(BF16), "in", scatter_dimension=0, tiled=True)
    u_all = lax.all_gather(ut, "in", axis=0)
    v_all = lax.all_gather(vt, "out", axis=0)
    blk = jnp.einsum("irt,ist->rs", u_all, v_all, preferred_element_type=F32).astype(BF16)
    row = lax.all_gather(blk, "in", axis=1, tiled=True)
    y = lax.dot_general(row, basis_in, (((1,), (1,)), ((), ())), preferred_element_type=F32)
    y_all = lax.all_gather(y.astype(BF16), "out", axis=0, tiled=True)
    gradient = lax.dot_general(
        lax.all_gather(cotangent, "in", axis=0, tiled=True),
        lax.all_gather(activations, "out", axis=0, tiled=True),
        (((0,), (0,)), ((), ())),
        preferred_element_type=F32,
    )
    return gradient - jnp.dot(basis_out, y_all, preferred_element_type=F32)


def solution(mesh):
    placed = (P("in", "out"), P("out", "in"), P("out", None), P("in", None))
    return jax.shard_map(
        body, mesh=mesh, in_specs=placed, out_specs=P("out", "in"), check_vma=False
    )
```

```python
import jax
import jax.numpy as jnp
from jax import lax
from jax.experimental import pallas as pl
from jax.experimental.pallas import tpu as pltpu
from jax.sharding import PartitionSpec as P

F32 = jnp.float32
BF16 = jnp.bfloat16
MESH = pl.DeviceIdType.MESH

TB = 128
BLK = 1024
NCOPY = 128


def rem(a, n):
    return lax.rem(a, jnp.int32(n))


def div(a, n):
    return lax.div(a, jnp.int32(n))


def rows(start, size):
    return pl.ds(pl.multiple_of(start, size), size)


def kernel(c_hbm, a_hbm, bo_hbm, bi_hbm, acc,
           call, aall, bo, bi, yall, st_u, rc_u0, st_u2, rc_u1,
           st_v, rc_v0, st_v2, rc_v1, uall, vall, ball, crow,
           load_sem, send_sem, recv_sem):
    o = lax.axis_index("out")
    i = lax.axis_index("in")
    c = rem(o, 2)
    xz = div(o, 2)
    x = div(o, 4)
    zl = rem(xz, 2)
    zh = div(i, 4)
    y = rem(i, 4)

    def dev(x_=None, zl_=None, c_=None, zh_=None, y_=None):
        x_ = x if x_ is None else x_
        zl_ = zl if zl_ is None else zl_
        c_ = c if c_ is None else c_
        zh_ = zh if zh_ is None else zh_
        y_ = y if y_ is None else y_
        return ((x_ * 2 + zl_) * 2 + c_, zh_ * 4 + y_)

    sib = dev(c_=1 - c)
    zl_peer = dev(zl_=1 - zl)

    def xz_dev(d):
        p = rem(xz + d, 8)
        return p, (p * 2 + c, i)

    def zh_dev(d):
        p = rem(zh + d, 4)
        return p, (o, p * 4 + y)

    def y_dev(d):
        p = rem(y + d, 4)
        return p, (o, zh * 4 + p)

    loads = [
        pltpu.make_async_copy(c_hbm, call.at[rows(i * TB, TB)], load_sem.at[0]),
        pltpu.make_async_copy(a_hbm, aall.at[rows(o * TB, TB)], load_sem.at[1]),
        pltpu.make_async_copy(bo_hbm, bo, load_sem.at[2]),
        pltpu.make_async_copy(bi_hbm, bi, load_sem.at[3]),
    ]
    for ld in loads:
        ld.start()

    barrier = pltpu.get_barrier_semaphore()
    partners = [sib] + [xz_dev(d)[1] for d in range(1, 8)]
    partners += [zh_dev(d)[1] for d in range(1, 4)] + [y_dev(d)[1] for d in range(1, 4)]
    for p in partners:
        pl.semaphore_signal(barrier, inc=1, device_id=p, device_id_type=MESH)

    made = []

    def remote(src, dst, device):
        n = len(made)
        cp = pltpu.make_async_remote_copy(
            src_ref=src, dst_ref=dst, send_sem=send_sem.at[n], recv_sem=recv_sem.at[n],
            device_id=device, device_id_type=MESH)
        made.append(cp)
        return cp

    def same(ref, device):
        return remote(ref, ref, device)

    def go(*cps):
        for cp in cps:
            cp.start()

    def got(*cps):
        for cp in cps:
            cp.wait_recv()

    class Ring:
        def __init__(self, buf, n, slot, pos, device):
            nxt, prv = rem(pos + 1, 4), rem(pos + 3, 4)
            h = n // 2
            up, down = device(nxt), device(prv)

            def half(p, k):
                return buf.at[rows(slot(p) * n + k * h, h)]

            self.f1 = same(half(pos, 0), up)
            self.b1 = same(half(pos, 1), down)
            self.f2 = same(half(pos, 1), up)
            self.b2 = same(half(pos, 0), down)
            self.f3 = same(half(prv, 0), up)
            self.b3 = same(half(nxt, 1), down)

        def s1(self):
            go(self.f1, self.b1)

        def s2(self):
            go(self.f2, self.b2)

        def s3(self):
            got(self.f1)
            go(self.f3)
            got(self.b1)
            go(self.b3)

        def near(self):
            got(self.f2, self.b2)

        def far(self):
            got(self.f3, self.b3)

    class OutGather:
        def __init__(self, buf, n):
            def blk(x_, zl_):
                return buf.at[rows(((x_ * 2 + zl_) * 2 + c) * n, n)]

            self.zl = same(blk(x, zl), zl_peer)
            self.own = Ring(buf, n, lambda p: (p * 2 + zl) * 2 + c, x, lambda p: dev(x_=p))
            self.pair = Ring(buf, n, lambda p: (p * 2 + 1 - zl) * 2 + c, x, lambda p: dev(x_=p))
            self.sibs = [same(blk(rem(x + d, 4), zl_), sib)
                         for d in (0, 1, 3, 2) for zl_ in (zl, 1 - zl)]

    cz = Ring(call, TB, lambda p: p * 4 + y, zh, lambda p: dev(zh_=p))
    qs = [rem(zh + d, 4) for d in (0, 3, 1, 2)]
    cy = [Ring(call, TB, lambda p, q=q: q * 4 + p, y, lambda p: dev(y_=p)) for q in qs]
    ag = OutGather(aall, TB)
    yg = OutGather(yall, 64)

    u_c = remote(st_u.at[1 - c], rc_u0, sib)
    u_x = []
    v_x = []
    for d in range(1, 8):
        p, device = xz_dev(d)
        u_x.append(remote(st_u2.at[p], rc_u1.at[d - 1], device))
    for d in range(1, 8):
        v_x.append(same(vall.at[c, xz], xz_dev(d)[1]))
    v_s = same(vall.at[c], sib)
    v_y = []
    v_z = []
    for d in range(1, 4):
        p, device = y_dev(d)
        v_y.append(remote(st_v.at[p], rc_v0.at[d - 1], device))
    for d in range(1, 4):
        p, device = zh_dev(d)
        v_z.append(remote(st_v2.at[p], rc_v1.at[d - 1], device))
    u_z = [same(uall.at[y, zh], zh_dev(d)[1]) for d in range(1, 4)]
    u_y = [same(uall.at[y], y_dev(d)[1]) for d in range(1, 4)]
    b_z = [same(ball.at[y, zh], zh_dev(d)[1]) for d in range(1, 4)]
    b_y = [same(ball.at[y], y_dev(d)[1]) for d in range(1, 4)]
    assert len(made) <= NCOPY

    def small(block, w):
        return lambda k: jnp.dot(
            block[...], w[:, k * 256:(k + 1) * 256], preferred_element_type=F32).T.astype(BF16)

    def grad(q, first):
        def step(j, carry):
            cols = pl.ds(pl.multiple_of(j * 256, 256), 256)
            lhs = call[rows(q * 512, 512), cols]
            part = lax.dot_general(lhs, aall[rows(q * 512, 512), :], (((0,), (0,)), ((), ())),
                                   preferred_element_type=F32)
            if first:
                acc[cols, :] = part
            else:
                acc[cols, :] += part
            return carry
        lax.fori_loop(0, 4, step, 0)

    def removal():
        def step(j, carry):
            r = pl.ds(pl.multiple_of(j * 256, 256), 256)
            acc[r, :] -= jnp.dot(bo[r, :], yall[...], preferred_element_type=F32)
            return carry
        lax.fori_loop(0, 4, step, 0)

    loads[0].wait()
    loads[1].wait()
    pl.semaphore_wait(barrier, len(partners))

    cz.s1()
    cy[0].s1()
    go(ag.zl, ag.sibs[0])
    ag.own.s1()
    cz.s2()

    loads[2].wait()
    part = small(call.at[rows(i * TB, TB)], bo)
    for k in range(4):
        t = part(k)
        for m in range(4):
            dst = k * 4 + m
            st_u[dst % 2, dst // 2] = t[m * 64:(m + 1) * 64, :]
    go(u_c)
    loads[3].wait()
    part = small(aall.at[rows(o * TB, TB)], bi)
    for k in range(4):
        t = part(k)
        for m in range(4):
            dst = k * 4 + m
            st_v[dst % 4, dst // 4] = t[m * 64:(m + 1) * 64, :]
    go(*v_y)

    cy[0].s2()
    ag.own.s2()
    got(ag.zl)
    go(ag.sibs[1])
    ag.pair.s1()

    got(u_c)
    st_u2[...] = (st_u[c].astype(F32) + rc_u0[...].astype(F32)).astype(BF16)
    go(*u_x)
    got(*v_y)
    st_v2[...] = (st_v[y].astype(F32) + rc_v0[0].astype(F32)
                  + rc_v0[1].astype(F32) + rc_v0[2].astype(F32)).astype(BF16)
    go(*v_z)

    cz.s3()
    cy[0].s3()
    ag.own.s3()
    ag.pair.s2()

    got(*u_x)
    total = st_u2[xz].astype(F32)
    for d in range(7):
        total += rc_u1[d].astype(F32)
    uall[y, zh] = total.astype(BF16)
    go(*u_z)
    got(*v_z)
    total = st_v2[zh].astype(F32)
    for d in range(3):
        total += rc_v1[d].astype(F32)
    vall[c, xz] = total.astype(BF16)
    go(*v_x)

    cz.near()
    cy[1].s1()
    ag.pair.s3()

    got(*u_z)
    go(*u_y)
    got(*v_x)
    go(v_s)

    cy[1].s2()

    got(*u_y)
    got(v_s)
    block = jnp.zeros((64, 128), F32)
    for t in range(16):
        v = vall[t % 2, t // 2]
        block += lax.dot_general(uall[t % 4, t // 4], jnp.concatenate([v, v], axis=0),
                                 (((1,), (1,)), ((), ())), preferred_element_type=F32)
    ball[y, zh] = block.astype(BF16)
    go(*b_z)

    cy[2].s1()
    ag.own.near()
    ag.pair.near()
    go(*ag.sibs[2:6])

    got(*b_z)
    go(*b_y)

    cy[1].s3()
    cy[2].s2()
    ag.own.far()
    ag.pair.far()
    go(*ag.sibs[6:8])

    got(*b_y)
    low = lax.broadcasted_iota(jnp.int32, (64, 128), 1) < 64
    for m in range(8):
        left = ball[(2 * m) % 4, m // 2].astype(F32)
        right = ball[(2 * m) % 4 + 1, m // 2].astype(F32)
        crow[:, m * 128:(m + 1) * 128] = jnp.where(low, left, right).astype(BF16)
    yall[rows(o * 64, 64), :] = lax.dot_general(
        crow[...], bi[...], (((1,), (1,)), ((), ())), preferred_element_type=F32).astype(BF16)
    go(yg.zl, yg.sibs[0])
    yg.own.s1()
    yg.own.s2()

    cy[2].s3()
    cz.far()
    cy[3].s1()
    cy[3].s2()

    got(*ag.sibs)
    cy[0].near()
    cy[0].far()
    got(yg.zl)
    go(yg.sibs[1])
    yg.pair.s1()
    yg.pair.s2()
    grad(qs[0], True)

    yg.own.s3()
    yg.pair.s3()
    cy[3].s3()
    cy[1].near()
    cy[1].far()
    grad(qs[1], False)

    yg.own.near()
    yg.pair.near()
    go(*yg.sibs[2:6])
    yg.own.far()
    yg.pair.far()
    go(*yg.sibs[6:8])
    cy[2].near()
    cy[2].far()
    grad(qs[2], False)
    got(*yg.sibs)
    removal()
    cy[3].near()
    cy[3].far()
    grad(qs[3], False)

    for cp in made:
        cp.wait_send()


def body(cotangent, activations, basis_out, basis_in):
    hbm = pl.BlockSpec(memory_space=pltpu.HBM)
    vm = pltpu.VMEM
    return pl.pallas_call(
        kernel,
        out_shape=jax.ShapeDtypeStruct((BLK, BLK), F32),
        in_specs=[hbm] * 4,
        out_specs=pl.BlockSpec(memory_space=pltpu.VMEM),
        scratch_shapes=[
            vm((16 * TB, BLK), BF16),
            vm((16 * TB, BLK), BF16),
            vm((BLK, 1024), BF16),
            vm((BLK, 1024), BF16),
            vm((1024, BLK), BF16),
            vm((2, 8, 64, 128), BF16),
            vm((8, 64, 128), BF16),
            vm((8, 64, 128), BF16),
            vm((7, 64, 128), BF16),
            vm((4, 4, 64, 128), BF16),
            vm((3, 4, 64, 128), BF16),
            vm((4, 64, 128), BF16),
            vm((3, 64, 128), BF16),
            vm((4, 4, 64, 128), BF16),
            vm((2, 8, 64, 128), BF16),
            vm((4, 4, 64, 128), BF16),
            vm((64, 1024), BF16),
            pltpu.SemaphoreType.DMA((4,)),
            pltpu.SemaphoreType.DMA((NCOPY,)),
            pltpu.SemaphoreType.DMA((NCOPY,)),
        ],
        compiler_params=pltpu.CompilerParams(
            collective_id=0, has_side_effects=True, vmem_limit_bytes=40 * 1024 * 1024),
        name="project",
    )(cotangent, activations, basis_out, basis_in)


def solution(mesh):
    placed = (P("in", "out"), P("out", "in"), P("out", None), P("in", None))
    return jax.shard_map(
        body, mesh=mesh, in_specs=placed, out_specs=P("out", "in"), check_vma=False
    )
```

```python
import functools

import jax
import jax.numpy as jnp
from jax import lax
from jax.experimental import pallas as pl
from jax.experimental.pallas import tpu as pltpu
from jax.sharding import PartitionSpec as P

F32 = jnp.float32
BF16 = jnp.bfloat16
MESH = pl.DeviceIdType.MESH

TB = 128
BLK = 1024
NCOPY = 152
DEPTH = 100

ORDER = (
    "V", "U", "go", "uc", "vy0", "vy1", "vy2", "azl0", "czb1", "as0", "aob1", "aof1", "pyb1",
    "U1", "ux0", "ux1", "ux2", "ux3", "ux4", "ux5", "ux6", "pyb2", "cy0b1", "czb2", "azl1",
    "aob2", "pyf1", "pyf2", "pyb3", "cy0f1", "cy0b2", "cwb1", "aof2", "pz0f1", "aob3", "V1",
    "vz0", "vz1", "vz2", "pyf3", "cy0b3", "cy0f2", "pz0b1", "aof3", "as1", "as2", "U2", "uz0",
    "uz1", "uz2", "apb1", "czb3", "cy0f3", "cy2b1", "as4", "czf1", "apf1", "cy2f2", "cwb2",
    "V2", "vx0", "vx1", "vx2", "vx3", "vx4", "vx5", "vx6", "as6", "apb2", "czf2", "cwb3", "uy0",
    "uy1", "uy2", "cy2b3", "pz0b2", "apf2", "apb3", "czf3", "pz0b3", "pz1b1", "pz1b2", "cy2b2",
    "cy2f1", "as3", "pz2b1", "apf3", "cwf1", "pz2b2", "vs", "pz3b1", "cy3b1", "pz3b2", "cy3f2",
    "as5", "B", "bz0", "bz1", "bz2", "pz1b3", "cwf2", "pz2b3", "cy2f3", "pz3b3", "as7", "cy1b2",
    "cwf3", "G00", "pz0f2", "by0", "by1", "by2", "G01", "pz0f3", "cy1b1", "G20", "pz1f1",
    "cy1f1", "G21", "pz1f2", "cy3b2", "pz2f1", "pz2f2", "cy1f2", "Y", "ys0", "yzl0", "yob1",
    "yof1", "yzl1", "yob2", "yof2", "cy1b3", "cy1f3", "cy3b3", "pz1f3", "ypf1", "ypb2", "yob3",
    "yof3", "pz2f3", "cy3f1", "pz3f1", "ypb1", "ys1", "ypf2", "ys2", "ys4", "pz3f2", "R00",
    "ypf3", "R01", "pz3f3", "ys6", "cy3f3", "ys5", "ypb3", "ys3", "G10", "G11", "R10", "R11",
    "R20", "ys7", "R21", "G30", "R30", "R31", "G31",
)

Q = 112


class Copy:
    def __init__(self, dma):
        self.dma = dma
        self.arrived = self.left = False

    def start(self):
        self.dma.start()

    def got(self):
        if not self.arrived:
            self.dma.wait_recv()
        self.arrived = True

    def sent(self):
        if not self.left:
            self.dma.wait_send()
        self.left = True


def rem(a, n):
    return lax.rem(a, jnp.int32(n))


def div(a, n):
    return lax.div(a, jnp.int32(n))


def rows(start, size):
    return pl.ds(pl.multiple_of(start, size), size)


LEGS = ("f1", "b1", "f2", "b2", "f3", "b3")


def LANE(name):
    axis = {"cz": "z", "cw": "z", "cy": "y", "py": "y", "pz": "z", "ao": "x", "ap": "x"}
    if name[:2] in axis:
        return axis[name[:2]] + name[-2]
    return ""


def dependencies():
    deps = {"V": [], "U": [], "uc": ["U"], "U1": ["U", "uc"], "V1": ["V", "vy0", "vy1", "vy2"],
            "U2": ["U1"] + [f"ux{k}" for k in range(7)],
            "V2": ["V1"] + [f"vz{k}" for k in range(3)],
            "B": ["U2", "V2", "vs"] + [f"vx{k}" for k in range(7)]
                 + [f"u{a}{k}" for a in "zy" for k in range(3)],
            "Y": ["B"] + [f"b{a}{k}" for a in "zy" for k in range(3)],
            "vs": ["V2"] + [f"vx{k}" for k in range(7)]}
    for tag, n, need in (("ux", 7, ["U1"]), ("vx", 7, ["V2"]), ("vy", 3, ["V"]),
                         ("vz", 3, ["V1"]), ("uz", 3, ["U2"]), ("bz", 3, ["B"]),
                         ("uy", 3, ["U2", "uz0", "uz1", "uz2"]),
                         ("by", 3, ["B", "bz0", "bz1", "bz2"])):
        for k in range(n):
            deps[f"{tag}{k}"] = need

    def ring(tag, half0, half1):
        deps.update({tag + "f1": half0, tag + "b1": half1, tag + "f2": half1,
                     tag + "b2": half0, tag + "f3": [tag + "f1"], tag + "b3": [tag + "b1"]})

    ring("cw", [], [])
    for first, then in (("cz", "cy"), ("py", "pz")):
        ring(first, [], [])
        for k, (p, q) in enumerate((("", ""), ("f1", "f2"), ("b2", "b1"), ("f3", "b3"))):
            both = [first, "cw"] if first == "cz" else [first]
            ring(f"{then}{k}", [f + p for f in both if p], [f + q for f in both if q])
    sides = ([], ["b1", "b2"], ["f1", "f2"], ["f3", "b3"])
    for tag, need in (("a", []), ("y", ["Y"])):
        zl = [tag + "zl0", tag + "zl1"]
        deps.update({zl[0]: need, zl[1]: need})
        ring(tag + "o", need, need)
        ring(tag + "p", zl[:1], zl[1:])
        for k, legs in enumerate(sides):
            deps[f"{tag}s{2 * k}"] = need + [f"{tag}o{leg}" for leg in legs]
            deps[f"{tag}s{2 * k + 1}"] = zl + [f"{tag}p{leg}" for leg in legs]
    every = [f"as{k}" for k in range(8)] + ["azl0", "azl1"] + [f"a{a}{leg}" for a in "op" for leg in LEGS]
    blocks = ([f"py{leg}" for leg in LEGS],
              [f"pz{k}{leg}" for k in range(4) for leg in ("f1", "f2")],
              [f"pz{k}{leg}" for k in range(4) for leg in ("b1", "b2")],
              [f"pz{k}{leg}" for k in range(4) for leg in ("f3", "b3")])
    come = ([], ["f1", "f2"], ["b1", "b2"], ["f3", "b3"])
    for k in range(4):
        for part in range(2):
            deps[f"G{k}{part}"] = (every + blocks[k] + [f"{f}{leg}" for leg in come[k] for f in ("cz", "cw")]
                                   + [f"cy{k}{leg}" for leg in LEGS])
            deps[f"R{k}{part}"] = ["Y", f"ys{2 * k}", f"ys{2 * k + 1}", "yzl0", "yzl1"] + [
                f"y{a}{leg}" for a in "op" for leg in sides[k]]
    return deps


def kernel(c_hbm, a_hbm, bo_hbm, bi_hbm, acc,
           call, aall, bo, bi, yall, st_u, rc_u0, st_u2, rc_u1,
           st_v, rc_v0, st_v2, rc_v1, uall, vall, ball, crow,
           load_sem, send_sem, recv_sem):
    o = lax.axis_index("out")
    i = lax.axis_index("in")
    c = rem(o, 2)
    xz = div(o, 2)
    x = div(o, 4)
    zl = rem(xz, 2)
    zh = div(i, 4)
    y = rem(i, 4)

    def dev(x_=None, zl_=None, c_=None, zh_=None, y_=None):
        x_ = x if x_ is None else x_
        zl_ = zl if zl_ is None else zl_
        c_ = c if c_ is None else c_
        zh_ = zh if zh_ is None else zh_
        y_ = y if y_ is None else y_
        return ((x_ * 2 + zl_) * 2 + c_, zh_ * 4 + y_)

    sib = dev(c_=1 - c)
    zl_peer = dev(zl_=1 - zl)

    def xz_dev(d):
        p = rem(xz + d, 8)
        return p, (p * 2 + c, i)

    def zh_dev(d):
        p = rem(zh + d, 4)
        return p, (o, p * 4 + y)

    def y_dev(d):
        p = rem(y + d, 4)
        return p, (o, zh * 4 + p)

    loads = [
        pltpu.make_async_copy(c_hbm, call.at[rows(i * TB, TB)], load_sem.at[0]),
        pltpu.make_async_copy(a_hbm, aall.at[rows(o * TB, TB)], load_sem.at[1]),
        pltpu.make_async_copy(bo_hbm, bo, load_sem.at[2]),
        pltpu.make_async_copy(bi_hbm, bi, load_sem.at[3]),
    ]
    for ld in loads:
        ld.start()

    barrier = pltpu.get_barrier_semaphore()
    partners = [sib] + [xz_dev(d)[1] for d in range(1, 8)]
    partners += [zh_dev(d)[1] for d in range(1, 4)] + [y_dev(d)[1] for d in range(1, 4)]
    for p in partners:
        pl.semaphore_signal(barrier, inc=1, device_id=p, device_id_type=MESH)

    made = []

    def remote(src, dst, device):
        n = len(made)
        cp = Copy(pltpu.make_async_remote_copy(
            src_ref=src, dst_ref=dst, send_sem=send_sem.at[n], recv_sem=recv_sem.at[n],
            device_id=device, device_id_type=MESH))
        made.append(cp)
        return cp

    def same(ref, device):
        return remote(ref, ref, device)

    class Ring:
        def __init__(self, buf, n, slot, pos, device, lo=0, hi=None):
            nxt, prv = rem(pos + 1, 4), rem(pos + 3, 4)
            size = (n if hi is None else hi) - lo
            up, down = device(nxt), device(prv)

            def half(p, k):
                return buf.at[pl.ds(pl.multiple_of(slot(p) * n + lo, 16), size),
                              pl.ds(k * 512, 512)]

            self.f1 = same(half(pos, 0), up)
            self.b1 = same(half(pos, 1), down)
            self.f2 = same(half(pos, 1), up)
            self.b2 = same(half(pos, 0), down)
            self.f3 = same(half(prv, 0), up)
            self.b3 = same(half(nxt, 1), down)

    class OutGather:
        def __init__(self, buf, n):
            def blk(x_, zl_):
                return buf.at[rows(((x_ * 2 + zl_) * 2 + c) * n, n)]

            self.zl = [same(buf.at[rows(((x * 2 + zl) * 2 + c) * n, n), pl.ds(k * 512, 512)],
                            zl_peer) for k in range(2)]
            self.own = Ring(buf, n, lambda p: (p * 2 + zl) * 2 + c, x, lambda p: dev(x_=p))
            self.pair = Ring(buf, n, lambda p: (p * 2 + 1 - zl) * 2 + c, x, lambda p: dev(x_=p))
            self.sibs = [same(blk(rem(x + d, 4), zl_), sib)
                         for d in (0, 1, 3, 2) for zl_ in (zl, 1 - zl)]

    near4 = (0, 3, 1, 2)
    qs = [rem(zh + d, 4) for d in near4]
    ys = [rem(y + d, 4) for d in near4]
    xs = [rem(x + d, 4) for d in (0, 1, 3, 2)]
    cz, cw = [Ring(call, TB, lambda p: p * 4 + y, zh, lambda p: dev(zh_=p), lo, hi)
              for lo, hi in ((0, 64), (64, Q))]
    cy = [Ring(call, TB, lambda p, q=q: q * 4 + p, y, lambda p: dev(y_=p), 0, Q) for q in qs]
    py = Ring(call, TB, lambda p: zh * 4 + p, y, lambda p: dev(y_=p), Q, TB)
    pz = [Ring(call, TB, lambda p, q=q: p * 4 + q, zh, lambda p: dev(zh_=p), Q, TB)
          for q in ys]
    ag = OutGather(aall, TB)
    yg = OutGather(yall, 64)

    u_c = remote(st_u.at[1 - c], rc_u0, sib)
    u_x = []
    v_x = []
    for d in range(1, 8):
        p, device = xz_dev(d)
        u_x.append(remote(st_u2.at[p], rc_u1.at[d - 1], device))
    for d in range(1, 8):
        v_x.append(same(vall.at[c, xz], xz_dev(d)[1]))
    v_s = same(vall.at[c], sib)
    v_y = []
    v_z = []
    for d in range(1, 4):
        p, device = y_dev(d)
        v_y.append(remote(st_v.at[p], rc_v0.at[d - 1], device))
    for d in range(1, 4):
        p, device = zh_dev(d)
        v_z.append(remote(st_v2.at[p], rc_v1.at[d - 1], device))
    u_z = [same(uall.at[y, zh], zh_dev(d)[1]) for d in range(1, 4)]
    u_y = [same(uall.at[y], y_dev(d)[1]) for d in range(1, 4)]
    b_z = [same(ball.at[y, zh], zh_dev(d)[1]) for d in range(1, 4)]
    b_y = [same(ball.at[y], y_dev(d)[1]) for d in range(1, 4)]
    assert len(made) <= NCOPY

    def small(block, w, put):
        for k in range(4):
            t = jnp.dot(block[...], w[:, k * 256:(k + 1) * 256],
                        preferred_element_type=F32).T.astype(BF16)
            for m in range(4):
                put(k * 4 + m, t[m * 64:(m + 1) * 64, :])

    written = set()

    def update(part, value, sign):
        first = part not in written
        written.add(part)

        def step(j, carry):
            r = rows(j * 256, 256)
            v = value(r)
            if first:
                acc[r, :] = v if sign > 0 else -v
            elif sign > 0:
                acc[r, :] += v
            else:
                acc[r, :] -= v
            return carry
        lax.fori_loop(2 * part, 2 * part + 2, step, 0)

    def grad(q, part):
        update(part, lambda r: lax.dot_general(
            call[rows(q * 512, 512), r], aall[rows(q * 512, 512), :],
            (((0,), (0,)), ((), ())), preferred_element_type=F32), 1)

    def removal(p, part):
        k = rows(p * 256, 256)
        update(part, lambda r: jnp.dot(bo[r, k], yall[k, :], preferred_element_type=F32), -1)

    def do_v():
        loads[3].wait()

        def put(n, piece):
            st_v[n % 4, n // 4] = piece
        small(aall.at[rows(o * TB, TB)], bi, put)

    def do_u():
        loads[2].wait()

        def put(n, piece):
            st_u[n % 2, n // 2] = piece
        small(call.at[rows(i * TB, TB)], bo, put)

    def do_u1():
        st_u2[...] = (st_u[c].astype(F32) + rc_u0[...].astype(F32)).astype(BF16)

    def do_v1():
        st_v2[...] = (st_v[y].astype(F32) + rc_v0[0].astype(F32)
                      + rc_v0[1].astype(F32) + rc_v0[2].astype(F32)).astype(BF16)

    def do_u2():
        total = st_u2[xz].astype(F32)
        for d in range(7):
            total += rc_u1[d].astype(F32)
        uall[y, zh] = total.astype(BF16)

    def do_v2():
        total = st_v2[zh].astype(F32)
        for d in range(3):
            total += rc_v1[d].astype(F32)
        vall[c, xz] = total.astype(BF16)

    def do_blk():
        block = jnp.zeros((64, 128), F32)
        for t in range(16):
            v = vall[t % 2, t // 2]
            block += lax.dot_general(uall[t % 4, t // 4], jnp.concatenate([v, v], axis=0),
                                     (((1,), (1,)), ((), ())), preferred_element_type=F32)
        low = lax.broadcasted_iota(jnp.int32, (32, 128), 1) < 64
        ball[y, zh] = jnp.where(low, block[:32], block[32:]).astype(BF16)

    def do_y():
        low = lax.broadcasted_iota(jnp.int32, (32, 128), 1) < 64
        for m in range(8):
            left = ball[(2 * m) % 4, m // 2].astype(F32)
            right = ball[(2 * m) % 4 + 1, m // 2].astype(F32)
            crow[:32, m * 128:(m + 1) * 128] = jnp.where(
                low, left, pltpu.roll(right, 64, 1)).astype(BF16)
            crow[32:, m * 128:(m + 1) * 128] = jnp.where(
                low, pltpu.roll(left, 64, 1), right).astype(BF16)
        yall[rows(o * 64, 64), :] = lax.dot_general(
            crow[...], bi[...], (((1,), (1,)), ((), ())), preferred_element_type=F32).astype(BF16)

    copies = {"uc": u_c, "vs": v_s}
    for tag, cps in (("ux", u_x), ("vx", v_x), ("vy", v_y), ("vz", v_z), ("uz", u_z),
                     ("uy", u_y), ("bz", b_z), ("by", b_y)):
        for k, cp in enumerate(cps):
            copies[f"{tag}{k}"] = cp
    rings = {"cz": cz, "cw": cw, "py": py, "ao": ag.own, "ap": ag.pair, "yo": yg.own, "yp": yg.pair}
    for k in range(4):
        rings[f"cy{k}"] = cy[k]
        rings[f"pz{k}"] = pz[k]
    for tag, r in rings.items():
        for leg in LEGS:
            copies[tag + leg] = getattr(r, leg)
    for tag, g in (("a", ag), ("y", yg)):
        for k in range(2):
            copies[f"{tag}zl{k}"] = g.zl[k]
        for k in range(8):
            copies[f"{tag}s{k}"] = g.sibs[k]
    assert len(copies) == len(made)
    work = {"V": do_v, "U": do_u, "U1": do_u1, "V1": do_v1, "U2": do_u2, "V2": do_v2,
            "B": do_blk, "Y": do_y}
    for k in range(4):
        for part in range(2):
            work[f"G{k}{part}"] = functools.partial(grad, qs[k], part)
            work[f"R{k}{part}"] = functools.partial(removal, xs[k], part)
    deps = dependencies()

    loads[0].wait()
    loads[1].wait()
    lanes = {}
    for name in ORDER:
        if name == "go":
            pl.semaphore_wait(barrier, len(partners))
            continue
        for d in deps[name]:
            if d in copies:
                copies[d].got()
        if name in work:
            work[name]()
            continue
        lane = lanes.setdefault(LANE(name), [])
        if LANE(name) and len(lane) >= DEPTH:
            lane[-DEPTH].sent()
        lane.append(copies[name])
        copies[name].start()
    assert len(set(ORDER)) == len(ORDER) == len(copies) + len(work) + 1

    for cp in made:
        cp.sent()


def body(cotangent, activations, basis_out, basis_in):
    hbm = pl.BlockSpec(memory_space=pltpu.HBM)
    vm = pltpu.VMEM
    return pl.pallas_call(
        kernel,
        out_shape=jax.ShapeDtypeStruct((BLK, BLK), F32),
        in_specs=[hbm] * 4,
        out_specs=pl.BlockSpec(memory_space=pltpu.VMEM),
        scratch_shapes=[
            vm((16 * TB, BLK), BF16),
            vm((16 * TB, BLK), BF16),
            vm((BLK, 1024), BF16),
            vm((BLK, 1024), BF16),
            vm((1024, BLK), BF16),
            vm((2, 8, 64, 128), BF16),
            vm((8, 64, 128), BF16),
            vm((8, 64, 128), BF16),
            vm((7, 64, 128), BF16),
            vm((4, 4, 64, 128), BF16),
            vm((3, 4, 64, 128), BF16),
            vm((4, 64, 128), BF16),
            vm((3, 64, 128), BF16),
            vm((4, 4, 64, 128), BF16),
            vm((2, 8, 64, 128), BF16),
            vm((4, 4, 32, 128), BF16),
            vm((64, 1024), BF16),
            pltpu.SemaphoreType.DMA((4,)),
            pltpu.SemaphoreType.DMA((NCOPY,)),
            pltpu.SemaphoreType.DMA((NCOPY,)),
        ],
        compiler_params=pltpu.CompilerParams(
            collective_id=0, has_side_effects=True, vmem_limit_bytes=40 * 1024 * 1024),
        name="project",
    )(*[pltpu.with_memory_space_constraint(v, pltpu.HBM)
        for v in (cotangent, activations, basis_out, basis_in)])


def solution(mesh):
    placed = (P("in", "out"), P("out", "in"), P("out", None), P("in", None))
    return jax.shard_map(
        body, mesh=mesh, in_specs=placed, out_specs=P("out", "in"), check_vma=False
    )
```

```python
import functools

import jax
import jax.numpy as jnp
from jax import lax
from jax.experimental import pallas as pl
from jax.experimental.pallas import tpu as pltpu
from jax.sharding import PartitionSpec as P

F32 = jnp.float32
BF16 = jnp.bfloat16
MESH = pl.DeviceIdType.MESH

TB = 128
BLK = 1024
NCOPY = 152
DEPTH = 100

ORDER = (
    "V", "U", "go", "azl1", "vy0", "czb1", "uc", "cwf1", "vy2", "cwb1", "aob1", "U1", "cy0f2",
    "ux4", "cwb2", "ux1", "ux3", "vy1", "ux5", "ux6", "ux2", "ux0", "aob2", "cy0f1", "aof1",
    "aof2", "czf1", "apf2", "cy0b1", "V1", "U2", "vz1", "uz2", "apb1", "uz1", "vz0", "cy0b2",
    "cy2f2", "aob3", "uz0", "azl0", "cy0f3", "vz2", "as2", "cy2b1", "aof3", "czb2", "V2", "vx3",
    "uy1", "vx6", "vx4", "czb3", "uy2", "vx0", "vx1", "as0", "vx2", "uy0", "vx5", "cy2b3",
    "cwf2", "cy0b3", "cy1f1", "cy2b2", "apf1", "cy2f1", "vs", "apb2", "cwb3", "B", "bz1", "bz0",
    "czf2", "apb3", "bz2", "apf3", "cy1f3", "by1", "cwf3", "as5", "czf3", "by2", "as1", "as6",
    "by0", "as3", "cy3b1", "as4", "cy2f3", "cy1b1", "as7", "cy1b2", "Y", "yof2", "yob1", "yof1",
    "yob2", "cy1f2", "yzl0", "G00", "yzl1", "G01", "cy1b3", "cy3b3", "yob3", "cy3f1", "ypb2",
    "cy3f2", "ys0", "ys2", "ypf1", "cy3b2", "G21", "ys4", "ypb1", "ys1", "ypf2", "G20", "R01",
    "yof3", "R00", "ys3", "ys5", "ypf3", "cy3f3", "ypb3", "R10", "R20", "G10", "ys6", "R11",
    "R21", "ys7", "G11", "R31", "R30", "G30", "G31",
)


class Copy:
    def __init__(self, dma):
        self.dma = dma
        self.arrived = self.left = False

    def start(self):
        self.dma.start()

    def got(self):
        if not self.arrived:
            self.dma.wait_recv()
        self.arrived = True

    def sent(self):
        if not self.left:
            self.dma.wait_send()
        self.left = True


def rem(a, n):
    return lax.rem(a, jnp.int32(n))


def div(a, n):
    return lax.div(a, jnp.int32(n))


def rows(start, size):
    return pl.ds(pl.multiple_of(start, size), size)


LEGS = ("f1", "b1", "f2", "b2", "f3", "b3")


def LANE(name):
    axis = {"cz": "z", "cw": "z", "cy": "y", "ao": "x", "ap": "x"}
    if name[:2] in axis:
        return axis[name[:2]] + name[-2]
    return ""


def dependencies():
    deps = {"V": [], "U": [], "uc": ["U"], "U1": ["U", "uc"], "V1": ["V", "vy0", "vy1", "vy2"],
            "U2": ["U1"] + [f"ux{k}" for k in range(7)],
            "V2": ["V1"] + [f"vz{k}" for k in range(3)],
            "B": ["U2", "V2", "vs"] + [f"vx{k}" for k in range(7)]
                 + [f"u{a}{k}" for a in "zy" for k in range(3)],
            "Y": ["B"] + [f"b{a}{k}" for a in "zy" for k in range(3)],
            "vs": ["V2"] + [f"vx{k}" for k in range(7)]}
    for tag, n, need in (("ux", 7, ["U1"]), ("vx", 7, ["V2"]), ("vy", 3, ["V"]),
                         ("vz", 3, ["V1"]), ("uz", 3, ["U2"]), ("bz", 3, ["B"]),
                         ("uy", 3, ["U2", "uz0", "uz1", "uz2"]),
                         ("by", 3, ["B", "bz0", "bz1", "bz2"])):
        for k in range(n):
            deps[f"{tag}{k}"] = need

    def ring(tag, half0, half1):
        deps.update({tag + "f1": half0, tag + "b1": half1, tag + "f2": half1,
                     tag + "b2": half0, tag + "f3": [tag + "f1"], tag + "b3": [tag + "b1"]})

    ring("cw", [], [])
    for first, then in (("cz", "cy"),):
        ring(first, [], [])
        for k, (p, q) in enumerate((("", ""), ("f1", "f2"), ("b2", "b1"), ("f3", "b3"))):
            both = [first, "cw"] if first == "cz" else [first]
            ring(f"{then}{k}", [f + p for f in both if p], [f + q for f in both if q])
    sides = ([], ["b1", "b2"], ["f1", "f2"], ["f3", "b3"])
    for tag, need in (("a", []), ("y", ["Y"])):
        zl = [tag + "zl0", tag + "zl1"]
        deps.update({zl[0]: need, zl[1]: need})
        ring(tag + "o", need, need)
        ring(tag + "p", zl[:1], zl[1:])
        for k, legs in enumerate(sides):
            deps[f"{tag}s{2 * k}"] = need + [f"{tag}o{leg}" for leg in legs]
            deps[f"{tag}s{2 * k + 1}"] = zl + [f"{tag}p{leg}" for leg in legs]
    every = [f"as{k}" for k in range(8)] + ["azl0", "azl1"] + [f"a{a}{leg}" for a in "op" for leg in LEGS]
    come = ([], ["f1", "f2"], ["b1", "b2"], ["f3", "b3"])
    for k in range(4):
        for part in range(2):
            deps[f"G{k}{part}"] = (every + [f"{f}{leg}" for leg in come[k] for f in ("cz", "cw")]
                                   + [f"cy{k}{leg}" for leg in LEGS])
            deps[f"R{k}{part}"] = ["Y", f"ys{2 * k}", f"ys{2 * k + 1}", "yzl0", "yzl1"] + [
                f"y{a}{leg}" for a in "op" for leg in sides[k]]
    return deps


def kernel(c_hbm, a_hbm, bo_hbm, bi_hbm, acc,
           call, aall, bo, bi, yall, st_u, rc_u0, st_u2, rc_u1,
           st_v, rc_v0, st_v2, rc_v1, uall, vall, ball, crow,
           load_sem, send_sem, recv_sem):
    o = lax.axis_index("out")
    i = lax.axis_index("in")
    c = rem(o, 2)
    xz = div(o, 2)
    x = div(o, 4)
    zl = rem(xz, 2)
    zh = div(i, 4)
    y = rem(i, 4)

    def dev(x_=None, zl_=None, c_=None, zh_=None, y_=None):
        x_ = x if x_ is None else x_
        zl_ = zl if zl_ is None else zl_
        c_ = c if c_ is None else c_
        zh_ = zh if zh_ is None else zh_
        y_ = y if y_ is None else y_
        return ((x_ * 2 + zl_) * 2 + c_, zh_ * 4 + y_)

    sib = dev(c_=1 - c)
    zl_peer = dev(zl_=1 - zl)

    def xz_dev(d):
        p = rem(xz + d, 8)
        return p, (p * 2 + c, i)

    def zh_dev(d):
        p = rem(zh + d, 4)
        return p, (o, p * 4 + y)

    def y_dev(d):
        p = rem(y + d, 4)
        return p, (o, zh * 4 + p)

    loads = [
        pltpu.make_async_copy(c_hbm, call.at[rows(i * TB, TB)], load_sem.at[0]),
        pltpu.make_async_copy(a_hbm, aall.at[rows(o * TB, TB)], load_sem.at[1]),
        pltpu.make_async_copy(bo_hbm, bo, load_sem.at[2]),
        pltpu.make_async_copy(bi_hbm, bi, load_sem.at[3]),
    ]
    for ld in loads:
        ld.start()

    barrier = pltpu.get_barrier_semaphore()
    partners = [sib] + [xz_dev(d)[1] for d in range(1, 8)]
    partners += [zh_dev(d)[1] for d in range(1, 4)] + [y_dev(d)[1] for d in range(1, 4)]
    for p in partners:
        pl.semaphore_signal(barrier, inc=1, device_id=p, device_id_type=MESH)

    made = []

    def remote(src, dst, device):
        n = len(made)
        cp = Copy(pltpu.make_async_remote_copy(
            src_ref=src, dst_ref=dst, send_sem=send_sem.at[n], recv_sem=recv_sem.at[n],
            device_id=device, device_id_type=MESH))
        made.append(cp)
        return cp

    def same(ref, device):
        return remote(ref, ref, device)

    class Ring:
        def __init__(self, buf, n, slot, pos, device, lo=0, hi=None):
            nxt, prv = rem(pos + 1, 4), rem(pos + 3, 4)
            size = (n if hi is None else hi) - lo
            up, down = device(nxt), device(prv)

            def half(p, k):
                return buf.at[pl.ds(pl.multiple_of(slot(p) * n + lo, 16), size),
                              pl.ds(k * 512, 512)]

            self.f1 = same(half(pos, 0), up)
            self.b1 = same(half(pos, 1), down)
            self.f2 = same(half(pos, 1), up)
            self.b2 = same(half(pos, 0), down)
            self.f3 = same(half(prv, 0), up)
            self.b3 = same(half(nxt, 1), down)

    class OutGather:
        def __init__(self, buf, n):
            def blk(x_, zl_):
                return buf.at[rows(((x_ * 2 + zl_) * 2 + c) * n, n)]

            self.zl = [same(buf.at[rows(((x * 2 + zl) * 2 + c) * n, n), pl.ds(k * 512, 512)],
                            zl_peer) for k in range(2)]
            self.own = Ring(buf, n, lambda p: (p * 2 + zl) * 2 + c, x, lambda p: dev(x_=p))
            self.pair = Ring(buf, n, lambda p: (p * 2 + 1 - zl) * 2 + c, x, lambda p: dev(x_=p))
            self.sibs = [same(blk(rem(x + d, 4), zl_), sib)
                         for d in (0, 1, 3, 2) for zl_ in (zl, 1 - zl)]

    near4 = (0, 3, 1, 2)
    qs = [rem(zh + d, 4) for d in near4]
    xs = [rem(x + d, 4) for d in (0, 1, 3, 2)]
    cz, cw = [Ring(call, TB, lambda p: p * 4 + y, zh, lambda p: dev(zh_=p), lo, hi)
              for lo, hi in ((0, 64), (64, TB))]
    cy = [Ring(call, TB, lambda p, q=q: q * 4 + p, y, lambda p: dev(y_=p), 0, TB) for q in qs]
    ag = OutGather(aall, TB)
    yg = OutGather(yall, 64)

    u_c = remote(st_u.at[1 - c], rc_u0, sib)
    u_x = []
    v_x = []
    for d in range(1, 8):
        p, device = xz_dev(d)
        u_x.append(remote(st_u2.at[p], rc_u1.at[d - 1], device))
    for d in range(1, 8):
        v_x.append(same(vall.at[c, xz], xz_dev(d)[1]))
    v_s = same(vall.at[c], sib)
    v_y = []
    v_z = []
    for d in range(1, 4):
        p, device = y_dev(d)
        v_y.append(remote(st_v.at[p], rc_v0.at[d - 1], device))
    for d in range(1, 4):
        p, device = zh_dev(d)
        v_z.append(remote(st_v2.at[p], rc_v1.at[d - 1], device))
    u_z = [same(uall.at[y, zh], zh_dev(d)[1]) for d in range(1, 4)]
    u_y = [same(uall.at[y], y_dev(d)[1]) for d in range(1, 4)]
    b_z = [same(ball.at[y, zh], zh_dev(d)[1]) for d in range(1, 4)]
    b_y = [same(ball.at[y], y_dev(d)[1]) for d in range(1, 4)]
    assert len(made) <= NCOPY

    def small(block, w, put):
        for k in range(4):
            t = jnp.dot(block[...], w[:, k * 256:(k + 1) * 256],
                        preferred_element_type=F32).T.astype(BF16)
            for m in range(4):
                put(k * 4 + m, t[m * 64:(m + 1) * 64, :])

    written = set()

    def update(part, value, sign):
        first = part not in written
        written.add(part)

        def step(j, carry):
            r = rows(j * 256, 256)
            v = value(r)
            if first:
                acc[r, :] = v if sign > 0 else -v
            elif sign > 0:
                acc[r, :] += v
            else:
                acc[r, :] -= v
            return carry
        lax.fori_loop(2 * part, 2 * part + 2, step, 0)

    def grad(q, part):
        update(part, lambda r: lax.dot_general(
            call[rows(q * 512, 512), r], aall[rows(q * 512, 512), :],
            (((0,), (0,)), ((), ())), preferred_element_type=F32), 1)

    def removal(p, part):
        k = rows(p * 256, 256)
        update(part, lambda r: jnp.dot(bo[r, k], yall[k, :], preferred_element_type=F32), -1)

    def do_v():
        loads[3].wait()

        def put(n, piece):
            st_v[n % 4, n // 4] = piece
        small(aall.at[rows(o * TB, TB)], bi, put)

    def do_u():
        loads[2].wait()

        def put(n, piece):
            st_u[n % 2, n // 2] = piece
        small(call.at[rows(i * TB, TB)], bo, put)

    def do_u1():
        st_u2[...] = (st_u[c].astype(F32) + rc_u0[...].astype(F32)).astype(BF16)

    def do_v1():
        st_v2[...] = (st_v[y].astype(F32) + rc_v0[0].astype(F32)
                      + rc_v0[1].astype(F32) + rc_v0[2].astype(F32)).astype(BF16)

    def do_u2():
        total = st_u2[xz].astype(F32)
        for d in range(7):
            total += rc_u1[d].astype(F32)
        uall[y, zh] = total.astype(BF16)

    def do_v2():
        total = st_v2[zh].astype(F32)
        for d in range(3):
            total += rc_v1[d].astype(F32)
        vall[c, xz] = total.astype(BF16)

    def do_blk():
        block = jnp.zeros((64, 128), F32)
        for t in range(16):
            v = vall[t % 2, t // 2]
            block += lax.dot_general(uall[t % 4, t // 4], jnp.concatenate([v, v], axis=0),
                                     (((1,), (1,)), ((), ())), preferred_element_type=F32)
        low = lax.broadcasted_iota(jnp.int32, (32, 128), 1) < 64
        ball[y, zh] = jnp.where(low, block[:32], block[32:]).astype(BF16)

    def do_y():
        low = lax.broadcasted_iota(jnp.int32, (32, 128), 1) < 64
        for m in range(8):
            left = ball[(2 * m) % 4, m // 2].astype(F32)
            right = ball[(2 * m) % 4 + 1, m // 2].astype(F32)
            crow[:32, m * 128:(m + 1) * 128] = jnp.where(
                low, left, pltpu.roll(right, 64, 1)).astype(BF16)
            crow[32:, m * 128:(m + 1) * 128] = jnp.where(
                low, pltpu.roll(left, 64, 1), right).astype(BF16)
        yall[rows(o * 64, 64), :] = lax.dot_general(
            crow[...], bi[...], (((1,), (1,)), ((), ())), preferred_element_type=F32).astype(BF16)

    copies = {"uc": u_c, "vs": v_s}
    for tag, cps in (("ux", u_x), ("vx", v_x), ("vy", v_y), ("vz", v_z), ("uz", u_z),
                     ("uy", u_y), ("bz", b_z), ("by", b_y)):
        for k, cp in enumerate(cps):
            copies[f"{tag}{k}"] = cp
    rings = {"cz": cz, "cw": cw, "ao": ag.own, "ap": ag.pair, "yo": yg.own, "yp": yg.pair}
    for k in range(4):
        rings[f"cy{k}"] = cy[k]
    for tag, r in rings.items():
        for leg in LEGS:
            copies[tag + leg] = getattr(r, leg)
    for tag, g in (("a", ag), ("y", yg)):
        for k in range(2):
            copies[f"{tag}zl{k}"] = g.zl[k]
        for k in range(8):
            copies[f"{tag}s{k}"] = g.sibs[k]
    assert len(copies) == len(made)
    work = {"V": do_v, "U": do_u, "U1": do_u1, "V1": do_v1, "U2": do_u2, "V2": do_v2,
            "B": do_blk, "Y": do_y}
    for k in range(4):
        for part in range(2):
            work[f"G{k}{part}"] = functools.partial(grad, qs[k], part)
            work[f"R{k}{part}"] = functools.partial(removal, xs[k], part)
    deps = dependencies()

    loads[0].wait()
    loads[1].wait()
    lanes = {}
    for name in ORDER:
        if name == "go":
            pl.semaphore_wait(barrier, len(partners))
            continue
        for d in deps[name]:
            if d in copies:
                copies[d].got()
        if name in work:
            work[name]()
            continue
        lane = lanes.setdefault(LANE(name), [])
        if LANE(name) and len(lane) >= DEPTH:
            lane[-DEPTH].sent()
        lane.append(copies[name])
        copies[name].start()
    assert len(set(ORDER)) == len(ORDER) == len(copies) + len(work) + 1

    for cp in made:
        cp.sent()


def body(cotangent, activations, basis_out, basis_in):
    hbm = pl.BlockSpec(memory_space=pltpu.HBM)
    vm = pltpu.VMEM
    return pl.pallas_call(
        kernel,
        out_shape=jax.ShapeDtypeStruct((BLK, BLK), F32),
        in_specs=[hbm] * 4,
        out_specs=pl.BlockSpec(memory_space=pltpu.VMEM),
        scratch_shapes=[
            vm((16 * TB, BLK), BF16),
            vm((16 * TB, BLK), BF16),
            vm((BLK, 1024), BF16),
            vm((BLK, 1024), BF16),
            vm((1024, BLK), BF16),
            vm((2, 8, 64, 128), BF16),
            vm((8, 64, 128), BF16),
            vm((8, 64, 128), BF16),
            vm((7, 64, 128), BF16),
            vm((4, 4, 64, 128), BF16),
            vm((3, 4, 64, 128), BF16),
            vm((4, 64, 128), BF16),
            vm((3, 64, 128), BF16),
            vm((4, 4, 64, 128), BF16),
            vm((2, 8, 64, 128), BF16),
            vm((4, 4, 32, 128), BF16),
            vm((64, 1024), BF16),
            pltpu.SemaphoreType.DMA((4,)),
            pltpu.SemaphoreType.DMA((NCOPY,)),
            pltpu.SemaphoreType.DMA((NCOPY,)),
        ],
        compiler_params=pltpu.CompilerParams(
            collective_id=0, has_side_effects=True, vmem_limit_bytes=40 * 1024 * 1024),
        name="project",
    )(*[pltpu.with_memory_space_constraint(v, pltpu.HBM)
        for v in (cotangent, activations, basis_out, basis_in)])


def solution(mesh):
    placed = (P("in", "out"), P("out", "in"), P("out", None), P("in", None))
    return jax.shard_map(
        body, mesh=mesh, in_specs=placed, out_specs=P("out", "in"), check_vma=False
    )
```
